256 devices in a mesh: dp: 8 (over x, y_lo), cent: 16 (over z, y_hi), rep: 2 (over core).
Axes of the slice: x: 4, y: 4 (y_hi: 2, y_lo: 2; y = y_hi * 2 + y_lo), z: 8, core: 2. Of those that a mesh axis runs over, the one named last changes fastest.
Arguments:
- rows: bfloat16 [32768, 1024], P(('dp', 'rep')), may hold values from -15 to 15
- panel: bfloat16 [16384, 1024], P('cent'), may hold values from -2.15 to 2.15
- scales: float32 [16384, 8], P('cent'), may hold values from 0.7 to 1.4
- inv_temp: int32 [1], replicated, may hold values from 4 to 15
Outputs:
- centroid_sums: float32 [1024, 16384], P(('dp', 'rep'), 'cent')
- centroid_counts: float32 [16384], P('cent')
The draws below stay inside these ranges and needn't reach their ends.
All inputs are finite; a program needn't handle non-finite values.
Results may differ from the reference program's by a relative error of at most 0.04.
Values may be sent and summed in bfloat16 or wider, within the bound.
No kernel may reach another device: no remote copies, remote signals or barrier semaphores. Data moves between devices by JAX's collectives and lax.ppermute only.
A program may use at most 64 MiB of HBM per device.

```python
import math
import jax
import jax.numpy as jnp
from jax import lax

D = 1024
BLOCK = 128
CENTROIDS = 16384
ROWS = 32768


def centroid_parts(key):
    signed = jax.random.uniform(jax.random.fold_in(key, 11), (CENTROIDS, D), jnp.float32, -1.0, 1.0)
    target = jnp.where(signed < 0.0, signed - 0.5, signed + 0.5)
    logs = jax.random.uniform(jax.random.fold_in(key, 12), (CENTROIDS, D // BLOCK), jnp.float32, math.log(0.7), math.log(1.4))
    scales = jnp.exp(logs)
    panel = (target.reshape(CENTROIDS, D // BLOCK, BLOCK) / scales[:, :, None]).reshape(CENTROIDS, D)
    return (panel, scales)


def draw_panel(key, part):
    panel, scales = centroid_parts(key)
    return panel.astype(jnp.bfloat16)


def draw_scales(key, part):
    panel, scales = centroid_parts(key)
    return scales


def draw_rows(key, part):
    panel, scales = centroid_parts(key)
    rounded = panel.astype(jnp.bfloat16).astype(jnp.float32)
    full = (rounded.reshape(CENTROIDS, D // BLOCK, BLOCK) * scales[:, :, None]).reshape(CENTROIDS, D)
    first = jax.random.randint(jax.random.fold_in(key, 23), (ROWS,), 0, CENTROIDS)
    strength = jax.random.uniform(jax.random.fold_in(key, 25), (ROWS, 1), jnp.float32, 1.0, 4.9)
    spread = jax.random.uniform(jax.random.fold_in(key, 24), (ROWS, 1), jnp.float32, 0.0, 3.0)
    extra = jnp.clip(jax.random.normal(jax.random.fold_in(key, 26), (ROWS, D), jnp.float32), -2.5, 2.5)
    mixed = strength * full[first] + spread * extra
    chosen = (jnp.arange(ROWS) % 64 == 0)[:, None]
    drawn = jnp.clip(jax.random.normal(jax.random.fold_in(key, 21), (ROWS, D), jnp.float32), -4.0, 4.0)
    values = jnp.where(chosen, mixed, drawn)
    return values.astype(jnp.bfloat16)


def setup_inputs(seed: int = 0) -> dict:
    streams_of = jax.random.split(jax.random.key(seed), 5)
    return {
        "rows": draw_rows(jax.random.fold_in(streams_of[4], 71), 0),
        "panel": draw_panel(jax.random.fold_in(streams_of[4], 71), 0),
        "scales": draw_scales(jax.random.fold_in(streams_of[4], 71), 0),
        "inv_temp": jax.random.randint(streams_of[3], (1,), 4, 16).astype(jnp.int32),
    }


def dequantize(panel, scales):
    count, width = panel.shape
    blocks = scales.shape[1]
    full = panel.astype(jnp.float32).reshape(count, blocks, width // blocks) * scales[:, :, None]
    return full.reshape(count, width).astype(jnp.bfloat16)

def reference(rows, panel, scales, inv_temp):
    centroids = dequantize(panel, scales)
    norms = lax.optimization_barrier(jnp.sum(centroids.astype(jnp.float32) ** 2, axis=1))
    factor = inv_temp[0].astype(jnp.float32) / math.sqrt(D)
    blk = math.gcd(ROWS, 512)
    stacked = rows.reshape(ROWS // blk, blk, D)

    def step(carry, row_block):
        prod = lax.dot_general(row_block, centroids, (((1,), (1,)), ((), ())), preferred_element_type=jnp.float32)
        logits = (prod - 0.5 * norms[None, :]) * factor
        row_max = lax.optimization_barrier(jnp.max(logits, axis=1))
        expo = jnp.exp(logits - row_max[:, None])
        row_total = lax.optimization_barrier(jnp.sum(expo, axis=1))
        weights = (expo / row_total[:, None]).astype(jnp.bfloat16)
        sums = carry[0] + lax.dot_general(row_block, weights, (((0,), (0,)), ((), ())), preferred_element_type=jnp.float32)
        counts = carry[1] + lax.optimization_barrier(jnp.sum(weights.astype(jnp.float32), axis=0))
        return ((sums, counts), None)
    init = (jnp.zeros((D, CENTROIDS), jnp.float32), jnp.zeros((CENTROIDS,), jnp.float32))
    (sums, counts), _ = lax.scan(step, init, stacked)
    return (sums, counts)
```

```python
import math

import jax
import jax.numpy as jnp
from jax import lax
from jax.experimental import pallas as pl
from jax.experimental.pallas import tpu as pltpu
from jax.sharding import PartitionSpec as P

BLOCK = 128
COLS = ((0, 384), (384, 768), (768, 1024))
RB = 256
EXTRA = 8
NT = (((1,), (1,)), ((), ()))
VMEM = pl.BlockSpec(memory_space=pltpu.VMEM)
SMEM = pl.BlockSpec(memory_space=pltpu.SMEM)
ANY = pl.BlockSpec(memory_space=pl.ANY)
PARAMS = pltpu.CompilerParams(vmem_limit_bytes=56 * 1024 * 1024)


def assign_kernel(
    fac_ref, scales_ref, panel_hbm, rows_hbm, expo_ref, stat_ref,
    panel, rows, cent, half, la, lb, psem, rsem,
):
    count, width = panel.shape
    total = rows.shape[0]
    kb = count // 4
    nrow = total // RB

    def pcopy(i):
        part = pl.ds(i * kb, kb)
        return pltpu.make_async_copy(panel_hbm.at[part], panel.at[part], psem.at[i])

    def rcopy(i):
        part = pl.ds(i * RB, RB)
        return pltpu.make_async_copy(rows_hbm.at[part], rows.at[part], rsem.at[i])

    for i in range(4):
        pcopy(i).start()
    for i in range(nrow):
        rcopy(i).start()
    cols = jnp.transpose(scales_ref[...])
    for i in range(4):
        pcopy(i).wait()
        norm = jnp.zeros((kb, BLOCK), jnp.float32)
        for b in range(width // BLOCK):
            x = panel[i * kb:(i + 1) * kb, b * BLOCK:(b + 1) * BLOCK].astype(jnp.float32)
            c = (x * cols[i * kb:(i + 1) * kb, b:b + 1]).astype(jnp.bfloat16)
            cent[i * kb:(i + 1) * kb, b * BLOCK:(b + 1) * BLOCK] = c
            c = c.astype(jnp.float32)
            norm = norm + c * c
        norm = 0.5 * jnp.sum(norm, axis=1, keepdims=True)
        half[i * kb:(i + 1) * kb, :] = jnp.broadcast_to(norm, (kb, BLOCK))
    fac = fac_ref[0]

    def product(i, out):
        part = pl.ds(pl.multiple_of(i * RB, RB), RB)
        out[...] = lax.dot_general(cent[...], rows[part, :], NT, preferred_element_type=jnp.float32)

    def soft(i, buf):
        tops, sums = [], []
        for t in range(RB // BLOCK):
            lanes = pl.ds(t * BLOCK, BLOCK)
            logits = (buf[:, lanes] - half[...]) * fac
            top = jnp.max(logits, axis=0, keepdims=True)
            expo = jnp.exp2(logits - top)
            out = pl.ds(pl.multiple_of(i * RB + t * BLOCK, BLOCK), BLOCK)
            expo_ref[:, out] = expo.astype(jnp.bfloat16)
            stat_ref[0:1, out] = top
            stat_ref[1:2, out] = top + jnp.log2(jnp.sum(expo, axis=0, keepdims=True))

    rcopy(0).wait()
    product(0, la)

    def pair(j, carry):
        i = 2 * j
        rcopy(i + 1).wait()
        product(i + 1, lb)
        soft(i, la)
        rcopy(i + 2).wait()
        product(i + 2, la)
        soft(i + 1, lb)
        return carry

    lax.fori_loop(0, nrow // 2 - 1, pair, 0)
    rcopy(nrow - 1).wait()
    product(nrow - 1, lb)
    soft(nrow - 2, la)
    soft(nrow - 1, lb)


def assign(rows, panel, scales_t, fac):
    total, width = rows.shape
    count = panel.shape[0]
    return pl.pallas_call(
        assign_kernel,
        out_shape=(
            jax.ShapeDtypeStruct((count, total), jnp.bfloat16),
            jax.ShapeDtypeStruct((2, total), jnp.float32),
        ),
        in_specs=[SMEM, VMEM, ANY, ANY],
        out_specs=(VMEM, VMEM),
        scratch_shapes=[
            pltpu.VMEM((count, width), jnp.bfloat16),
            pltpu.VMEM((total, width), jnp.bfloat16),
            pltpu.VMEM((count, width), jnp.bfloat16),
            pltpu.VMEM((count, BLOCK), jnp.float32),
            pltpu.VMEM((count, RB), jnp.float32),
            pltpu.VMEM((count, RB), jnp.float32),
            pltpu.SemaphoreType.DMA((4,)),
            pltpu.SemaphoreType.DMA((total // RB,)),
        ],
        compiler_params=PARAMS,
        cost_estimate=pl.CostEstimate(
            flops=2 * total * width * count, bytes_accessed=10 * 1024 * 1024, transcendentals=total * count
        ),
        name="assign",
    )(fac, scales_t, panel, rows)


def flip_kernel(place_ref, rows_ref, out_ref):
    total, width = rows_ref.shape
    for t in range(width // 128):
        turned = jnp.transpose(rows_ref[:, t * 128:(t + 1) * 128])
        for r in range(2):
            at = pl.multiple_of(place_ref[2 * t + r], 64)
            out_ref[pl.ds(at, 64), :] = turned[r * 64:(r + 1) * 64, :]
    out_ref[width:, :] = jnp.ones((EXTRA, total), jnp.bfloat16)


def flip(rows, place):
    total, width = rows.shape
    return pl.pallas_call(
        flip_kernel,
        out_shape=jax.ShapeDtypeStruct((width + EXTRA, total), jnp.bfloat16),
        in_specs=[SMEM, VMEM],
        out_specs=VMEM,
        compiler_params=PARAMS,
        cost_estimate=pl.CostEstimate(flops=0, bytes_accessed=8 * 1024 * 1024, transcendentals=0),
        name="flip",
    )(place, rows)


def order(j):
    spots = []
    for p in range(8):
        bits = [(p >> 2) & 1, (p >> 1) & 1, p & 1]
        bits = bits[j:] + bits[:j]
        spots.append(bits[0] * 4 + bits[1] * 2 + bits[2])
    return spots


def counted(block):
    hi = block.astype(jnp.bfloat16).astype(jnp.float32)
    row = lax.broadcasted_iota(jnp.int32, block.shape, 0)
    return jnp.where(row % 2 == 0, hi, block - hi)


def rounded(block):
    hi = block.astype(jnp.bfloat16).astype(jnp.float32)
    return hi + (block - hi).astype(jnp.bfloat16).astype(jnp.float32)


def sums_kernel(stat_ref, lse_ref, lhs_ref, expo_ref, send_ref, keep_ref):
    width = lhs_ref.shape[0] - EXTRA
    half = width // 2
    scale = jnp.exp2(stat_ref[0:1, :] - lse_ref[...])
    for j, (a, b) in enumerate(COLS):
        w = (expo_ref[a:b, :].astype(jnp.float32) * scale).astype(jnp.bfloat16)
        acc = lax.dot_general(lhs_ref[...], w, NT, preferred_element_type=jnp.float32)
        for p, q in enumerate(order(j)):
            keep_ref[q * 64:(q + 1) * 64, a:b] = acc[p * 64:(p + 1) * 64, :]
            send_ref[q * 64:(q + 1) * 64, a:b] = acc[half + p * 64:half + (p + 1) * 64, :].astype(jnp.bfloat16)
        keep_ref[half:, a:b] = acc[width:, :]
        send_ref[half:, a:b] = counted(acc[width:, :]).astype(jnp.bfloat16)


def weighted(stat, lse, lhs, expo):
    half = (lhs.shape[0] - EXTRA) // 2
    count = expo.shape[0]
    return pl.pallas_call(
        sums_kernel,
        out_shape=(
            jax.ShapeDtypeStruct((half + EXTRA, count), jnp.bfloat16),
            jax.ShapeDtypeStruct((half + EXTRA, count), jnp.float32),
        ),
        in_specs=[VMEM] * 4,
        out_specs=(VMEM, VMEM),
        compiler_params=PARAMS,
        cost_estimate=pl.CostEstimate(
            flops=2 * lhs.shape[0] * lhs.shape[1] * count, bytes_accessed=12 * 1024 * 1024, transcendentals=2048
        ),
        name="sums",
    )(stat, lse, lhs, expo)


def added(keep, recv):
    h = keep.shape[0] - EXTRA
    total = keep[:h, :] + recv[:h, :].astype(jnp.float32)
    got = recv[h:, :].astype(jnp.float32)
    other = got[0:1, :] + got[1:2, :]
    return total, rounded(keep[h:, :]) + other


def fold(keeps, recvs):
    n = len(keeps)
    h = (keeps[0].shape[0] - EXTRA) // 2

    def kernel(*refs):
        for j in range(n):
            total, count = added(refs[j], refs[n + j])
            send, keep = refs[2 * n + 2 * j], refs[2 * n + 2 * j + 1]
            keep[:h, :] = total[:h, :]
            keep[h:, :] = count
            send[:h, :] = total[h:, :].astype(jnp.bfloat16)
            send[h:, :] = counted(count).astype(jnp.bfloat16)

    shapes = []
    for k in keeps:
        shapes += [
            jax.ShapeDtypeStruct((h + EXTRA, k.shape[1]), jnp.bfloat16),
            jax.ShapeDtypeStruct((h + EXTRA, k.shape[1]), jnp.float32),
        ]
    out = pl.pallas_call(
        kernel, out_shape=shapes, in_specs=[VMEM] * (2 * n), out_specs=[VMEM] * (2 * n),
        compiler_params=PARAMS, name="fold",
    )(*keeps, *recvs)
    return out[0::2], out[1::2]


def split(keep, recv):
    n = len(COLS)
    h = (keep.shape[0] - EXTRA) // 2

    def kernel(keep_ref, recv_ref, *outs):
        for j, (a, b) in enumerate(COLS):
            total, count = added(keep_ref[:, a:b], recv_ref[:, a:b])
            outs[2 * j + 1][:h, :] = total[:h, :]
            outs[2 * j + 1][h:, :] = count
            outs[2 * j][:h, :] = total[h:, :].astype(jnp.bfloat16)
            outs[2 * j][h:, :] = counted(count).astype(jnp.bfloat16)

    shapes = []
    for a, b in COLS:
        shapes += [
            jax.ShapeDtypeStruct((h + EXTRA, b - a), jnp.bfloat16),
            jax.ShapeDtypeStruct((h + EXTRA, b - a), jnp.float32),
        ]
    out = pl.pallas_call(
        kernel, out_shape=shapes, in_specs=[VMEM] * 2, out_specs=[VMEM] * (2 * n),
        compiler_params=PARAMS, name="split",
    )(keep, recv)
    return out[0::2], out[1::2]


def finish(keeps, recvs):
    n = len(keeps)
    h = keeps[0].shape[0] - EXTRA
    count = COLS[-1][1]

    def kernel(*refs):
        for j, (a, b) in enumerate(COLS):
            total, cnt = added(refs[j], refs[n + j])
            refs[2 * n][:, a:b] = total
            refs[2 * n + 1][:, a:b] = cnt[0:1, :]

    return pl.pallas_call(
        kernel,
        out_shape=(jax.ShapeDtypeStruct((h, count), jnp.float32), jax.ShapeDtypeStruct((1, count), jnp.float32)),
        in_specs=[VMEM] * (2 * n), out_specs=(VMEM, VMEM), compiler_params=PARAMS, name="finish",
    )(*keeps, *recvs)


def joined(parts):
    top = parts[0]
    for p in parts[1:]:
        top = jnp.maximum(top, p)
    total = jnp.exp2(parts[0] - top)
    for p in parts[1:]:
        total = total + jnp.exp2(p - top)
    return top + jnp.log2(total)


def cent_move(x, dz, dh):
    pairs = [(z * 2 + h, ((z + dz) % 8) * 2 + (h ^ dh)) for z in range(8) for h in range(2)]
    return lax.ppermute(x, "cent", pairs)


def flipped(x, axis, n, mask):
    return lax.ppermute(x, axis, [(i, i ^ mask) for i in range(n)])


def on_device(rows, panel, scales, inv_temp):
    width = rows.shape[1]
    fac = inv_temp.astype(jnp.float32) * (math.log2(math.e) / math.sqrt(width))
    expo, stat = assign(rows, panel, scales.T, fac)

    dp, rep = lax.axis_index("dp"), lax.axis_index("rep")
    x, y = dp // 2, dp % 2
    code = y * 4 + jnp.where((x == 1) | (x == 2), 2, 0) + jnp.where(x >= 2, 1, 0)
    place = []
    for t in range(8):
        tx, ty = t // 2, t % 2
        theirs = ty * 4 + (2 if tx in (1, 2) else 0) + (1 if tx >= 2 else 0)
        spot = (code ^ theirs) * 64
        place += [spot + 512 * rep, spot + 512 * (1 - rep)]
    place = jnp.stack(place).astype(jnp.int32)
    lhs = flip(rows, place)

    lse = stat[1:2]
    lse = joined([lse, cent_move(lse, 1, 0), cent_move(lse, -1, 0), cent_move(lse, 0, 1)])
    lse = joined([lse, cent_move(lse, 4, 0), cent_move(lse, 2, 1), cent_move(lse, -2, 1)])

    send, keep = weighted(stat, lse, lhs, expo)
    sends, keeps = split(keep, flipped(send, "rep", 2, 1))
    masks = (1, 2, 6)
    for s in range(3):
        recvs = [flipped(c, "dp", 8, masks[(j + s) % 3]) for j, c in enumerate(sends)]
        if s < 2:
            sends, keeps = fold(keeps, recvs)
    sums, counts = finish(keeps, recvs)
    return (sums, counts[0])


def solution(mesh):
    in_specs = (P(("dp", "rep"), None), P("cent", None), P("cent", None), P())
    out_specs = (P(("dp", "rep"), "cent"), P("cent"))
    return jax.shard_map(
        on_device, mesh=mesh, in_specs=in_specs, out_specs=out_specs, check_vma=False
    )
```

```python
import math

import jax
import jax.numpy as jnp
from jax import lax
from jax.experimental import pallas as pl
from jax.experimental.pallas import tpu as pltpu
from jax.sharding import PartitionSpec as P

BLOCK = 128
RB = 512
KB = 256
SB = 128
SPLIT = 2
EXTRA = 8
PARTS = 2
NT = (((1,), (1,)), ((), ()))
VMEM = pl.BlockSpec(memory_space=pltpu.VMEM)
SMEM = pl.BlockSpec(memory_space=pltpu.SMEM)
HBM = pl.BlockSpec(memory_space=pltpu.HBM)


def limit(mib):
    return pltpu.CompilerParams(vmem_limit_bytes=mib * 1024 * 1024)


def assign_kernel(
    fac_ref, scales_ref, panel_hbm, rows_hbm, expo_ref, top_ref, lse_ref,
    panel, rows, cent, half, psem, rsem,
):
    count, width = panel.shape
    total = rows.shape[0]
    nk, nr = count // KB, total // RB

    def pcopy(i):
        part = pl.ds(i * KB, KB)
        return pltpu.make_async_copy(panel_hbm.at[part], panel.at[part], psem.at[i])

    def rcopy(i):
        part = pl.ds(i * RB, RB)
        return pltpu.make_async_copy(rows_hbm.at[part], rows.at[part], rsem.at[i])

    pcopy(0).start()
    pcopy(1).start()
    rcopy(0).start()
    for i in range(2, nk):
        pcopy(i).start()
    for i in range(1, nr):
        rcopy(i).start()
    cols = jnp.transpose(scales_ref[...])
    fac = fac_ref[0]

    def dequantize(i):
        ks = slice(i * KB, (i + 1) * KB)
        norm = None
        for b in range(width // BLOCK):
            ds = slice(b * BLOCK, (b + 1) * BLOCK)
            c = (panel[ks, ds].astype(jnp.float32) * cols[ks, b:b + 1]).astype(jnp.bfloat16)
            cent[ks, ds] = c
            c = c.astype(jnp.float32)
            norm = c * c if norm is None else norm + c * c
        norm = 0.5 * jnp.sum(norm, axis=1, keepdims=True)
        half[ks, :] = jnp.broadcast_to(norm, (KB, BLOCK))

    def product(i, first, size):
        ks = slice(first, first + size)
        at = slice(i * RB, (i + 1) * RB)
        expo_ref[ks, at] = lax.dot_general(
            cent[ks, :], rows[at, :], NT, preferred_element_type=jnp.float32
        )

    def soft(i, t):
        at = slice(i * RB + t * BLOCK, i * RB + (t + 1) * BLOCK)
        top = jnp.full((8, BLOCK), -jnp.inf, jnp.float32)
        for g in range(0, count, SB):
            ks = slice(g, g + SB)
            dist = (expo_ref[ks, at] - half[ks, :]).reshape(SB // 8, 8, BLOCK)
            top = jnp.maximum(top, jnp.max(dist, axis=0))
        top = jnp.max(top, axis=0, keepdims=True)
        tot = jnp.zeros((8, BLOCK), jnp.float32)
        for g in range(0, count, SB):
            ks = slice(g, g + SB)
            expo = jnp.exp2(((expo_ref[ks, at] - half[ks, :]) - top) * fac)
            expo_ref[ks, at] = expo
            tot = tot + jnp.sum(expo.reshape(SB // 8, 8, BLOCK), axis=0)
        top = top * fac
        top_ref[:, at] = top
        lse_ref[:, at] = top + jnp.log2(jnp.sum(tot, axis=0, keepdims=True))

    pcopy(0).wait()
    dequantize(0)
    for i in range(1, nk):
        pcopy(i).wait()
    rcopy(0).wait()
    for i in range(nk):
        product(0, i * KB, KB)
        if i + 1 < nk:
            dequantize(i + 1)
    for i in range(1, nr):
        rcopy(i).wait()
    tiles = RB // BLOCK
    for i in range(1, nr):
        for j in range(SPLIT):
            product(i, j * count // SPLIT, count // SPLIT)
            for t in range(j * tiles // SPLIT, (j + 1) * tiles // SPLIT):
                soft(i - 1, t)
    for t in range(tiles):
        soft(nr - 1, t)


def assign(rows, panel, scales_t, fac):
    total, width = rows.shape
    count = panel.shape[0]
    line = jax.ShapeDtypeStruct((1, total), jnp.float32)
    return pl.pallas_call(
        assign_kernel,
        out_shape=(jax.ShapeDtypeStruct((count, total), jnp.float32), line, line),
        in_specs=[SMEM, VMEM, HBM, HBM],
        out_specs=(VMEM, VMEM, VMEM),
        scratch_shapes=[
            pltpu.VMEM((count, width), jnp.bfloat16),
            pltpu.VMEM((total, width), jnp.bfloat16),
            pltpu.VMEM((count, width), jnp.bfloat16),
            pltpu.VMEM((count, BLOCK), jnp.float32),
            pltpu.SemaphoreType.DMA((count // KB,)),
            pltpu.SemaphoreType.DMA((total // RB,)),
        ],
        compiler_params=limit(24),
        cost_estimate=pl.CostEstimate(
            flops=2 * total * width * count, bytes_accessed=10 * 1024 * 1024, transcendentals=total * count
        ),
        name="assign",
    )(fac, scales_t, *(pltpu.with_memory_space_constraint(x, pltpu.HBM) for x in (panel, rows)))


def bits_of(x, y):
    one, two = x % 2, x // 2
    return y, one + two - 2 * one * two, two


def flip_kernel(rows_ref, out_ref):
    total, width = rows_ref.shape
    dp, rep = lax.axis_index("dp"), lax.axis_index("rep")
    mine = bits_of(dp // 2, dp % 2)
    for t in range(width // 128):
        turned = jnp.transpose(rows_ref[:, t * 128:(t + 1) * 128])
        y, a, b = [m + o - 2 * m * o for m, o in zip(mine, bits_of(t // 2, t % 2))]
        for r, spot in enumerate((4 * y + 2 * a + b, 4 * a + 2 * b + y)):
            other = rep + r - 2 * rep * r
            at = pl.multiple_of(spot * 64 + other * (width // 2), 64)
            out_ref[pl.ds(at, 64), :] = turned[r * 64:(r + 1) * 64, :]
    out_ref[width:, :] = jnp.ones((EXTRA, total), jnp.bfloat16)


def flip(rows, part):
    total, width = rows.shape
    total = total // 2
    return pl.pallas_call(
        flip_kernel,
        grid=(1,),
        out_shape=jax.ShapeDtypeStruct((width + EXTRA, total), jnp.bfloat16),
        in_specs=[pl.BlockSpec((total, width), lambda i: (part, 0))],
        out_specs=VMEM,
        compiler_params=limit(14),
        cost_estimate=pl.CostEstimate(flops=0, bytes_accessed=4 * 1024 * 1024, transcendentals=0),
        name="flip",
    )(rows)


def join(parts):
    def kernel(*refs):
        vals = [r[...] for r in refs[:-1]]
        top = vals[0]
        for v in vals[1:]:
            top = jnp.maximum(top, v)
        total = jnp.exp2(vals[0] - top)
        for v in vals[1:]:
            total = total + jnp.exp2(v - top)
        refs[-1][...] = top + jnp.log2(total)

    return pl.pallas_call(
        kernel, out_shape=jax.ShapeDtypeStruct(parts[0].shape, jnp.float32),
        in_specs=[VMEM] * len(parts), out_specs=VMEM, compiler_params=limit(2), name="join",
    )(*parts)


def counted(block):
    hi = block.astype(jnp.bfloat16).astype(jnp.float32)
    row = lax.broadcasted_iota(jnp.int32, block.shape, 0)
    return jnp.where(row % 2 == 0, hi, block - hi).astype(jnp.bfloat16)


def rounded(block):
    hi = block.astype(jnp.bfloat16).astype(jnp.float32)
    return hi + (block - hi).astype(jnp.bfloat16).astype(jnp.float32)


def sums_kernel(part, top_ref, lse_ref, lhs0_ref, lhs1_ref, expo_ref, send_ref, keep_ref):
    width = lhs0_ref.shape[0] - EXTRA
    half = width // 2
    cols = send_ref.shape[1]
    scale = jnp.exp2(top_ref[...] - lse_ref[...])
    acc = None
    n = lhs0_ref.shape[1]
    for j, lhs in enumerate((lhs0_ref, lhs1_ref)):
        ex = expo_ref[part * cols:(part + 1) * cols, j * n:(j + 1) * n]
        w = (ex * scale[:, j * n:(j + 1) * n]).astype(jnp.bfloat16)
        one = lax.dot_general(lhs[...], w, NT, preferred_element_type=jnp.float32)
        acc = one if acc is None else acc + one
    keep_ref[:half, :] = acc[:half, :]
    keep_ref[half:, :] = acc[width:, :]
    send_ref[:half, :] = acc[half:width, :].astype(jnp.bfloat16)
    send_ref[half:, :] = counted(acc[width:, :])


def weighted(part, top, lse, lhs0, lhs1, expo):
    half = (lhs0.shape[0] - EXTRA) // 2
    cols = expo.shape[0] // PARTS

    def kernel(*refs):
        sums_kernel(part, *refs)

    return pl.pallas_call(
        kernel,
        out_shape=(
            jax.ShapeDtypeStruct((half + EXTRA, cols), jnp.bfloat16),
            jax.ShapeDtypeStruct((half + EXTRA, cols), jnp.float32),
        ),
        in_specs=[VMEM] * 5,
        out_specs=(VMEM, VMEM),
        compiler_params=limit(16),
        cost_estimate=pl.CostEstimate(
            flops=2 * lhs0.shape[0] * expo.shape[1] * cols, bytes_accessed=1024 * 1024, transcendentals=2048
        ),
        name="sums",
    )(top, lse, lhs0, lhs1, expo)


def added(keep, recv):
    h = keep.shape[0] - EXTRA
    total = keep[:h, :] + recv[:h, :].astype(jnp.float32)
    got = recv[h:, :].astype(jnp.float32)
    return total, rounded(keep[h:, :]) + (got[0:1, :] + got[1:2, :])


def fold(keep, recv):
    h = (keep.shape[0] - EXTRA) // 2

    def kernel(keep_ref, recv_ref, send_ref, next_ref):
        total, count = added(keep_ref, recv_ref)
        next_ref[:h, :] = total[:h, :]
        next_ref[h:, :] = count
        send_ref[:h, :] = total[h:, :].astype(jnp.bfloat16)
        send_ref[h:, :] = counted(count)

    shape = (h + EXTRA, keep.shape[1])
    return pl.pallas_call(
        kernel,
        out_shape=(jax.ShapeDtypeStruct(shape, jnp.bfloat16), jax.ShapeDtypeStruct(shape, jnp.float32)),
        in_specs=[VMEM] * 2, out_specs=(VMEM, VMEM), compiler_params=limit(4), name="fold",
    )(keep, recv)


def finish(keeps, recvs):
    n = len(keeps)
    h = keeps[0].shape[0] - EXTRA
    cols = keeps[0].shape[1]

    def kernel(*refs):
        for j in range(n):
            total, count = added(refs[j], refs[n + j])
            refs[2 * n][:, j * cols:(j + 1) * cols] = total
            refs[2 * n + 1][:, j * cols:(j + 1) * cols] = count[0:1, :]

    return pl.pallas_call(
        kernel,
        out_shape=(
            jax.ShapeDtypeStruct((h, n * cols), jnp.float32),
            jax.ShapeDtypeStruct((1, n * cols), jnp.float32),
        ),
        in_specs=[VMEM] * (2 * n), out_specs=(VMEM, VMEM), compiler_params=limit(4), name="finish",
    )(*keeps, *recvs)


def cent_move(x, dz, dh):
    pairs = [(z * 2 + h, ((z + dz) % 8) * 2 + (h ^ dh)) for z in range(8) for h in range(2)]
    return lax.ppermute(x, "cent", pairs)


def swap(x):
    return lax.ppermute(x, "rep", [(0, 1), (1, 0)])


def exchange(x, step):
    masks = ((1, 2, 6), (2, 6, 1))
    pairs = [(d * 2 + r, (d ^ masks[r][step]) * 2 + r) for d in range(8) for r in range(2)]
    return lax.ppermute(x, ("dp", "rep"), pairs)


def on_device(rows, panel, scales, inv_temp):
    width = rows.shape[1]
    fac = inv_temp.astype(jnp.float32) * (math.log2(math.e) / math.sqrt(width))
    expo, top, lse = assign(rows, panel, scales.T, fac)
    lhs0 = flip(rows, 0)
    lhs1 = flip(rows, 1)

    lse = join([lse, cent_move(lse, 1, 0), cent_move(lse, -1, 0), cent_move(lse, 0, 1)])
    lse = join([lse, cent_move(lse, 4, 0), cent_move(lse, 2, 1), cent_move(lse, -2, 1)])

    pairs = [weighted(j, top, lse, lhs0, lhs1, expo) for j in range(PARTS)]
    sends, keeps = [p[0] for p in pairs], [p[1] for p in pairs]
    recvs = [swap(s) for s in sends]
    for step in range(3):
        pairs = [fold(k, r) for k, r in zip(keeps, recvs)]
        sends, keeps = [p[0] for p in pairs], [p[1] for p in pairs]
        recvs = [exchange(s, step) for s in sends]
    sums, counts = finish(keeps, recvs)
    return (sums, counts[0])


def solution(mesh):
    in_specs = (P(("dp", "rep"), None), P("cent", None), P("cent", None), P())
    out_specs = (P(("dp", "rep"), "cent"), P("cent"))
    return jax.shard_map(
        on_device, mesh=mesh, in_specs=in_specs, out_specs=out_specs, check_vma=False
    )
```
